32 devices in a mesh: slab: 4 (over x, core), dom: 8 (over z, y).
Axes of the slice: x: 2, y: 2, z: 4, core: 2. Of those that a mesh axis runs over, the one named last changes fastest.
Arguments:
- donors: bfloat16 [262144, 128], P(('slab', 'dom')), may hold values from -6 to 6
- send_block: int32 [4, 8, 8, 8], P('slab', 'dom'), may hold values from 0 to 63
- send_count: int32 [4, 8, 8], P('slab', 'dom'), may hold values from 1 to 8, as said below
- send_target: int32 [4, 8, 8, 8], P('slab', 'dom'), may hold values from 0 to 1
- target_block: int32 [4, 8, 8, 2], P('slab', 'dom'), may hold values from 0 to 7
- weights: bfloat16 [4, 8, 8, 8, 128, 128], P('slab', 'dom'), may hold values from -0.25 to 0.25
- halo_weights: bfloat16 [4, 8, 2, 128, 128], P('slab', 'dom'), may hold values from -0.375 to 0.375
- permute: int32 [4, 8, 1024], P('slab', 'dom'), may hold values from 0 to 1023, each once within a row
Outputs:
- balanced: bfloat16 [32768, 128], P(('slab', 'dom'))
The draws below stay inside these ranges and needn't reach their ends.
Inputs may be any that keep to these rules, and one draw needn't show every extreme that they name: `send_count`: each source has at least one destination with exactly 8 live slots.
All inputs are finite; a program needn't handle non-finite values.
Results may differ from the reference program's by a relative error of at most 0.0047.
Values may be sent and summed in bfloat16 or wider, within the bound.
No kernel may reach another device: no remote copies, remote signals or barrier semaphores. Data moves between devices by JAX's collectives and lax.ppermute only.
A program may use at most 128 MiB of HBM per device.

```python
import jax
import jax.numpy as jnp
from jax import lax

V = 128
BR = 128
NB_DEV = 64
NEW_DEV = 8
CAP = 8
PT = 2
HB = 2
DONOR_ROWS = 262144
N_SLAB = 4
N_DOM = 8


def draw_send_count(key, part):
    first, second = jax.random.split(jax.random.fold_in(key, 11))
    counts = jax.random.randint(first, (N_SLAB, N_DOM, N_DOM), 1, CAP + 1)
    hot = jax.random.randint(second, (N_SLAB, N_DOM, 1), 0, N_DOM)
    lanes = jnp.arange(N_DOM)[None, None, :]
    return jnp.where(lanes == hot, CAP, counts).astype(jnp.int32)


def touch_ends(values, own_key, least, top_value):
    longest = values.shape.index(max(values.shape))
    spots = []
    for shift in (0, 1):
        where = [jax.random.randint(jax.random.fold_in(own_key, axis), (), 0, length) for axis, length in enumerate(values.shape)]
        where[longest] = (where[longest] + shift) % values.shape[longest]
        spots.append(tuple(where))
    return values.at[spots[0]].set(least).at[spots[1]].set(top_value)


def steps_of(stream_key, shape, cuts, smallest, high):
    factor_of, own = 1.0, jax.random.fold_in(stream_key, 6)
    for position, blocks in cuts:
        steps = jnp.exp(jax.random.uniform(jax.random.fold_in(own, position), (blocks,), jnp.float32, smallest / len(cuts), high / len(cuts)))
        factor_of = factor_of * jnp.repeat(steps, shape[position] // blocks).reshape([-1 if axis == position else 1 for axis in range(len(shape))])
    return factor_of


def gaussian(own_key, shape, scale, limit, cuts=(), kind=jnp.bfloat16):
    entries = jax.random.normal(own_key, shape, jnp.float32) * scale
    if len(cuts) > 0:
        entries = steps_of(own_key, shape, cuts, -0.22, 0.18) * entries
    return jnp.clip(entries, min=-limit, max=limit).astype(kind)


def setup_inputs(seed: int = 0) -> dict:
    key_list = jax.random.split(jax.random.key(seed), 9)
    donors = gaussian(key_list[0], (DONOR_ROWS, V), 1.0, 6.0, ((0, 32),))
    send_block = touch_ends(jax.random.randint(key_list[1], (N_SLAB, N_DOM, N_DOM, CAP), 0, NB_DEV), jax.random.fold_in(key_list[1], 1), 0, NB_DEV - 1).astype(jnp.int32)
    send_count = draw_send_count(jax.random.fold_in(key_list[8], 71), 0)
    send_target = touch_ends(jax.random.randint(key_list[3], (N_SLAB, N_DOM, N_DOM, CAP), 0, PT), jax.random.fold_in(key_list[3], 1), 0, PT - 1).astype(jnp.int32)
    target_block = touch_ends(jax.random.randint(key_list[4], (N_SLAB, N_DOM, N_DOM, PT), 0, NEW_DEV), jax.random.fold_in(key_list[4], 1), 0, NEW_DEV - 1).astype(jnp.int32)
    weights = gaussian(key_list[5], (N_SLAB, N_DOM, N_DOM, CAP, BR, BR), (BR * N_DOM * CAP // (2 * NEW_DEV)) ** -0.5, 0.25, ((0, 4), (1, 8)))
    halo_weights = gaussian(key_list[6], (N_SLAB, N_DOM, HB, BR, BR), (BR * HB) ** -0.5, 0.375, ((0, 4), (1, 8)))
    permute = jax.vmap(lambda own: jax.random.permutation(own, NEW_DEV * BR))(jax.random.split(key_list[7], N_SLAB * N_DOM)).reshape((N_SLAB, N_DOM, NEW_DEV * BR)).astype(jnp.int32)
    return dict(donors=donors, send_block=send_block, send_count=send_count, send_target=send_target, target_block=target_block, weights=weights, halo_weights=halo_weights, permute=permute)


def reference(donors, send_block, send_count, send_target, target_block, weights, halo_weights, permute):
    hp = lax.Precision.HIGHEST
    blocks = donors.reshape(N_SLAB, N_DOM, NB_DEV, BR, V)
    previous = jnp.concatenate([jnp.zeros_like(blocks[:1]), blocks[:-1]], 0)
    rims = previous[:, :, NB_DEV - HB:]
    share = (NEW_DEV * BR) // N_DOM

    def one_slab(slab_id):
        slab_blocks = blocks[slab_id]

        def add_source(total, source):
            picked = slab_blocks[source][send_block[slab_id, source]]
            live = jnp.arange(CAP)[None, :] < send_count[slab_id, source][:, None]
            choose = (send_target[slab_id, source][:, :, None] == jnp.arange(PT)[None, None, :]) & live[:, :, None]
            prods = jnp.einsum("pcij,pcjv->pciv", weights[slab_id, source].astype(jnp.float32), picked.astype(jnp.float32), precision=hp)
            parts = jnp.einsum("pct,pciv->ptiv", choose.astype(jnp.float32), prods, precision=hp).astype(jnp.bfloat16)
            placer = (target_block[slab_id][:, source][:, :, None] == jnp.arange(NEW_DEV)[None, None, :]).astype(jnp.float32)
            total = total + jnp.einsum("ptj,ptiv->pjiv", placer, parts.astype(jnp.float32), precision=hp)
            return total, None

        start = jnp.zeros((N_DOM, NEW_DEV, BR, V), jnp.float32)
        total, _ = lax.scan(add_source, start, jnp.arange(N_DOM))
        halo_term = jnp.einsum("phij,phjv->piv", halo_weights[slab_id].astype(jnp.float32), rims[slab_id].astype(jnp.float32), precision=hp)
        total = total.at[:, 0].add(halo_term)
        rows = total.astype(jnp.bfloat16).reshape(N_DOM, NEW_DEV * BR, V)
        ordered = jnp.take_along_axis(rows, permute[slab_id][:, :, None], axis=1)
        moved = ordered.reshape(N_DOM, N_DOM, share, V).transpose(1, 0, 2, 3)
        return moved.reshape(N_DOM * NEW_DEV * BR, V)

    result = lax.map(one_slab, jnp.arange(N_SLAB))
    return result.reshape(N_SLAB * N_DOM * NEW_DEV * BR, V)
```

```python
import jax
import jax.numpy as jnp
from jax import lax
from jax.experimental import pallas as pl
from jax.experimental.pallas import tpu as pltpu
from jax.sharding import PartitionSpec as P


def parts_kernel(block_of, count_of, target_of, donors, weights, out, held_w, held_d, sem_w, sem_d):
    n_dest, capacity = block_of.shape
    rows = held_w.shape[2]
    places = out.shape[1]

    def start(p, carry):
        pltpu.make_async_copy(weights.at[p], held_w.at[p], sem_w.at[p]).start()
        for c in range(capacity):
            row = pl.multiple_of(block_of[p, c] * rows, rows)
            pltpu.make_async_copy(
                donors.at[pl.ds(row, rows)], held_d.at[p, pl.ds(c * rows, rows)], sem_d.at[p]
            ).start()
        return carry

    lax.fori_loop(0, n_dest, start, 0)

    def work(p, carry):
        pltpu.make_async_copy(weights.at[p], held_w.at[p], sem_w.at[p]).wait()
        pltpu.make_async_copy(held_d.at[p], held_d.at[p], sem_d.at[p]).wait()
        total = None
        for c in range(0, capacity, 2):
            left = jnp.concatenate([held_w[p, c], held_w[p, c + 1]], axis=1)
            pieces = []
            for k in (c, c + 1):
                block = held_d[p, pl.ds(k * rows, rows)]
                live = k < count_of[p]
                kept = []
                for t in range(places):
                    wanted = jnp.logical_and(live, target_of[p, k] == t)
                    kept.append(jnp.where(wanted, block, jnp.zeros_like(block)))
                pieces.append(jnp.concatenate(kept, axis=1))
            right = jnp.concatenate(pieces, axis=0)
            prod = jnp.dot(left, right, preferred_element_type=jnp.float32)
            total = prod if total is None else total + prod
        width = out.shape[-1]
        for t in range(places):
            out[p, t] = total[:, t * width : (t + 1) * width].astype(out.dtype)
        return carry

    lax.fori_loop(0, n_dest, work, 0)


def form_parts(slots, counts, targets, donors, weights, places):
    n_dest, capacity, rows, _ = weights.shape
    width = donors.shape[1]
    smem = pl.BlockSpec(memory_space=pltpu.SMEM)
    hbm = pl.BlockSpec(memory_space=pl.ANY)
    return pl.pallas_call(
        parts_kernel,
        out_shape=jax.ShapeDtypeStruct((n_dest, places, rows, width), jnp.bfloat16),
        in_specs=[smem, smem, smem, hbm, hbm],
        out_specs=pl.BlockSpec(memory_space=pltpu.VMEM),
        scratch_shapes=[
            pltpu.VMEM((n_dest, capacity, rows, rows), weights.dtype),
            pltpu.VMEM((n_dest, capacity * rows, width), donors.dtype),
            pltpu.SemaphoreType.DMA((n_dest,)),
            pltpu.SemaphoreType.DMA((n_dest,)),
        ],
        name="parts",
    )(slots, counts, targets, donors, weights)


def place_kernel(place_of, parts, halo_w, rim, order, out, fresh):
    n_src, places = place_of.shape
    rows, width = parts.shape[2:]
    total_rows = fresh.shape[0]
    halo = jnp.zeros((rows, width), jnp.float32)
    for h in range(halo_w.shape[0]):
        halo += jnp.dot(halo_w[h], rim[h], preferred_element_type=jnp.float32)
    fresh[pl.ds(0, rows)] = halo
    fresh[pl.ds(rows, total_rows - rows)] = jnp.zeros((total_rows - rows, width), jnp.float32)

    def add(q, carry):
        for t in range(places):
            row = pl.multiple_of(place_of[q, t] * rows, rows)
            fresh[pl.ds(row, rows)] += parts[q, t].astype(jnp.float32)
        return carry

    lax.fori_loop(0, n_src, add, 0)
    values = fresh[...].astype(jnp.bfloat16)
    lane = lax.broadcasted_iota(jnp.int32, (rows, total_rows), 1)

    def pick(j, carry):
        wanted = jnp.broadcast_to(order[pl.ds(j, 1), :], (rows, rows)).T
        wanted = jnp.concatenate([wanted] * (total_rows // rows), axis=1)
        chosen = jnp.where(lane == wanted, 1.0, 0.0).astype(jnp.bfloat16)
        row = pl.multiple_of(j * rows, rows)
        out[pl.ds(row, rows)] = jnp.dot(
            chosen, values, preferred_element_type=jnp.float32
        ).astype(out.dtype)
        return carry

    lax.fori_loop(0, total_rows // rows, pick, 0)


def place_parts(places_of, parts, halo_w, rim, order):
    rows, width = parts.shape[2:]
    total_rows = order.size
    smem = pl.BlockSpec(memory_space=pltpu.SMEM)
    vmem = pl.BlockSpec(memory_space=pltpu.VMEM)
    return pl.pallas_call(
        place_kernel,
        out_shape=jax.ShapeDtypeStruct((total_rows, width), jnp.bfloat16),
        in_specs=[smem, vmem, vmem, vmem, vmem],
        out_specs=vmem,
        scratch_shapes=[pltpu.VMEM((total_rows, width), jnp.float32)],
        name="place",
    )(places_of, parts, halo_w, rim, order)


def on_device(
    donors, send_block, send_count, send_target, target_block, weights, halo_weights, permute
):
    block_rows = weights.shape[-1]
    width = donors.shape[1]
    rim_count = halo_weights.shape[2]
    slabs = lax.axis_size("slab")
    rim = lax.ppermute(
        donors[donors.shape[0] - rim_count * block_rows :].reshape(rim_count, block_rows, width),
        "slab",
        [(source, source + 1) for source in range(slabs - 1)],
    )
    parts = form_parts(
        send_block[0, 0], send_count[0, 0], send_target[0, 0], donors, weights[0, 0],
        target_block.shape[-1],
    )
    arrived = lax.all_to_all(parts, "dom", split_axis=0, concat_axis=0, tiled=True)
    ordered = place_parts(
        target_block[0, 0], arrived, halo_weights[0, 0], rim, permute[0, 0].reshape(-1, block_rows)
    )
    return lax.all_to_all(ordered, "dom", split_axis=0, concat_axis=0, tiled=True)


def solution(mesh):
    return jax.shard_map(
        on_device,
        mesh=mesh,
        in_specs=(
            P(("slab", "dom"), None),
            P("slab", "dom", None, None),
            P("slab", "dom", None),
            P("slab", "dom", None, None),
            P("slab", "dom", None, None),
            P("slab", "dom", None, None, None, None),
            P("slab", "dom", None, None, None),
            P("slab", "dom", None),
        ),
        out_specs=P(("slab", "dom"), None),
        check_vma=False,
    )
```

```python
import functools

import jax
import jax.numpy as jnp
from jax import lax
from jax.experimental import pallas as pl
from jax.experimental.pallas import tpu as pltpu
from jax.sharding import PartitionSpec as P


VMEM = pl.BlockSpec(memory_space=pltpu.VMEM)
SMEM = pl.BlockSpec(memory_space=pltpu.SMEM)
HBM = pl.BlockSpec(memory_space=pltpu.HBM)
MARGIN = 4 << 20


def nbytes(*arrays):
    return sum(a.size * jnp.dtype(a.dtype).itemsize for a in arrays)


def partner(me, step, count):
    if count & (count - 1) == 0:
        return jnp.bitwise_xor(me, step)
    return lax.rem(me + step, count)


def giver(me, step, count):
    if count & (count - 1) == 0:
        return jnp.bitwise_xor(me, step)
    return lax.rem(me + count - step, count)


def send(value, step):
    count = lax.axis_size("dom")
    if count & (count - 1) == 0:
        pairs = [(source, source ^ step) for source in range(count)]
    else:
        pairs = [(source, (source + step) % count) for source in range(count)]
    return lax.ppermute(value, "dom", pairs)


def parts_kernel(steps, count, load, *refs):
    block_hbm, count_hbm, target_hbm, donors, weights = refs[:5]
    outs = refs[5 : 5 + len(steps)]
    extra = refs[5 + len(steps)]
    held_d = extra if load else donors
    block_of, count_of, target_of, held_w, sems, sem_w = refs[-6:]
    rows = held_w.shape[2]
    capacity = held_w.shape[1]
    width = held_d.shape[1]
    places = outs[0].shape[0] // rows
    me = lax.axis_index("dom")
    owners = [partner(me, step, count) for step in steps]
    tables = [
        pltpu.make_async_copy(block_hbm, block_of, sems.at[0]),
        pltpu.make_async_copy(count_hbm, count_of, sems.at[1]),
        pltpu.make_async_copy(target_hbm, target_of, sems.at[2]),
    ]
    if load:
        tables.append(pltpu.make_async_copy(donors, held_d, sems.at[3]))
    loads = [
        pltpu.make_async_copy(weights.at[p], held_w.at[i], sem_w.at[i])
        for i, p in enumerate(owners)
    ]
    for copy in tables + loads:
        copy.start()
    for copy in tables:
        copy.wait()
    for i, p in enumerate(owners):
        loads[i].wait()
        total = None
        for c in range(0, capacity, 2):
            left = jnp.concatenate([held_w[i, c], held_w[i, c + 1]], axis=1)
            pieces = []
            for k in (c, c + 1):
                row = pl.multiple_of(block_of[p, k] * rows, rows)
                block = held_d[pl.ds(row, rows)]
                live = k < count_of[p]
                kept = []
                for t in range(places):
                    wanted = jnp.logical_and(live, target_of[p, k] == t)
                    kept.append(jnp.where(wanted, block, jnp.zeros_like(block)))
                pieces.append(jnp.concatenate(kept, axis=1))
            right = jnp.concatenate(pieces, axis=0)
            prod = jnp.dot(left, right, preferred_element_type=jnp.float32)
            total = prod if total is None else total + prod
        for t in range(places):
            outs[i][t * rows : (t + 1) * rows] = total[:, t * width : (t + 1) * width].astype(
                outs[i].dtype
            )
    if not load:
        extra[...] = held_d[held_d.shape[0] - extra.shape[0] : held_d.shape[0]]


def form_parts(steps, tables, donors, weights, places, load, extra_rows):
    n_dest, capacity, rows, _ = weights.shape
    width = donors.shape[1]
    shapes = [jax.ShapeDtypeStruct((places * rows, width), jnp.bfloat16)] * len(steps)
    shapes.append(jax.ShapeDtypeStruct((extra_rows, width), donors.dtype))
    in_hbm = functools.partial(pltpu.with_memory_space_constraint, memory_space=pltpu.HBM)
    held = jax.ShapeDtypeStruct((len(steps), capacity, rows, rows), weights.dtype)
    return pl.pallas_call(
        functools.partial(parts_kernel, steps, n_dest, load),
        out_shape=shapes,
        in_specs=[HBM, HBM, HBM, HBM if load else VMEM, HBM],
        out_specs=[VMEM] * len(shapes),
        scratch_shapes=[pltpu.SMEM(table.shape, table.dtype) for table in tables]
        + [
            pltpu.VMEM(held.shape, held.dtype),
            pltpu.SemaphoreType.DMA((4,)),
            pltpu.SemaphoreType.DMA((len(steps),)),
        ],
        compiler_params=pltpu.CompilerParams(
            vmem_limit_bytes=nbytes(held, donors, *shapes) + MARGIN
        ),
        cost_estimate=pl.CostEstimate(
            flops=4 * len(steps) * capacity * rows * rows * width,
            bytes_accessed=nbytes(held, donors),
            transcendentals=0,
        ),
        name="parts",
    )(*map(in_hbm, tables), in_hbm(donors) if load else donors, in_hbm(weights))


def prep_kernel(order, halo_w, rim, chosen, halo):
    rows = order.shape[1]
    total_rows = chosen.shape[1]
    blocks = total_rows // rows
    total = None
    for h in range(halo_w.shape[0]):
        prod = jnp.dot(
            halo_w[h], rim[h * rows : (h + 1) * rows], preferred_element_type=jnp.float32
        )
        total = prod if total is None else total + prod
    halo[...] = total
    lane = lax.broadcasted_iota(jnp.int32, (rows, rows), 1)

    def pick(j, carry):
        wanted = jnp.broadcast_to(order[pl.ds(j, 1), :], (rows, rows)).T
        row = pl.multiple_of(j * rows, rows)
        for b in range(blocks):
            chosen[pl.ds(row, rows), b * rows : (b + 1) * rows] = jnp.where(
                lane + b * rows == wanted, 1.0, 0.0
            ).astype(jnp.bfloat16)
        return carry

    lax.fori_loop(0, blocks, pick, 0)


def prepare(order, halo_w, rim):
    total_rows = order.size
    shapes = (
        jax.ShapeDtypeStruct((total_rows, total_rows), jnp.bfloat16),
        jax.ShapeDtypeStruct((halo_w.shape[1], rim.shape[1]), jnp.float32),
    )
    return pl.pallas_call(
        prep_kernel,
        out_shape=shapes,
        in_specs=[VMEM, VMEM, VMEM],
        out_specs=(VMEM, VMEM),
        compiler_params=pltpu.CompilerParams(
            vmem_limit_bytes=nbytes(order, halo_w, rim, *shapes) + MARGIN
        ),
        cost_estimate=pl.CostEstimate(
            flops=total_rows * total_rows, bytes_accessed=8 << 20, transcendentals=0
        ),
        name="prep",
    )(order, halo_w, rim)


def place_kernel(steps, count, place_of, chosen, halo, *refs):
    parts = refs[: len(steps)]
    outs = refs[len(steps) : 2 * len(steps)]
    fresh = refs[-1]
    rows, width = halo.shape
    total_rows = fresh.shape[0]
    places = parts[0].shape[0] // rows
    me = lax.axis_index("dom")
    fresh[0:rows] = halo[...]
    fresh[rows:total_rows] = jnp.zeros((total_rows - rows, width), jnp.float32)
    for step, part in zip(steps, parts):
        q = giver(me, step, count)
        for t in range(places):
            row = pl.multiple_of(place_of[t, q] * rows, rows)
            fresh[pl.ds(row, rows)] += part[t * rows : (t + 1) * rows].astype(jnp.float32)
    values = fresh[...].astype(jnp.bfloat16)
    share = total_rows // count
    for step, out in zip(steps, outs):
        row = pl.multiple_of(partner(me, step, count) * share, share)
        out[...] = jnp.dot(
            chosen[pl.ds(row, share)], values, preferred_element_type=jnp.float32
        ).astype(out.dtype)


def place_parts(steps, count, places_of, chosen, halo, parts):
    total_rows = chosen.shape[0]
    width = halo.shape[1]
    shapes = [jax.ShapeDtypeStruct((total_rows // count, width), jnp.bfloat16)] * len(steps)
    fresh = jax.ShapeDtypeStruct((total_rows, width), jnp.float32)
    return pl.pallas_call(
        functools.partial(place_kernel, steps, count),
        out_shape=shapes,
        in_specs=[SMEM] + [VMEM] * (2 + len(parts)),
        out_specs=[VMEM] * len(shapes),
        scratch_shapes=[pltpu.VMEM(fresh.shape, fresh.dtype)],
        compiler_params=pltpu.CompilerParams(
            vmem_limit_bytes=nbytes(chosen, halo, fresh, *parts, *shapes) + MARGIN
        ),
        cost_estimate=pl.CostEstimate(
            flops=2 * total_rows * total_rows * width, bytes_accessed=4 << 20, transcendentals=0
        ),
        name="place",
    )(places_of, chosen, halo, *parts)


def join_kernel(steps, count, *refs):
    chunks = refs[: len(steps)]
    out, sem = refs[len(steps) :]
    me = lax.axis_index("dom")
    copies = []
    for step, chunk in zip(steps, chunks):
        share = chunk.shape[0]
        row = pl.multiple_of(giver(me, step, count) * share, share)
        copies.append(pltpu.make_async_copy(chunk, out.at[pl.ds(row, share)], sem))
    for copy in copies:
        copy.start()
    for copy in copies:
        copy.wait()


def join(steps, count, chunks):
    share, width = chunks[0].shape
    return pl.pallas_call(
        functools.partial(join_kernel, steps, count),
        out_shape=jax.ShapeDtypeStruct((share * len(chunks), width), chunks[0].dtype),
        in_specs=[VMEM] * len(chunks),
        out_specs=HBM,
        scratch_shapes=[pltpu.SemaphoreType.DMA(())],
        compiler_params=pltpu.CompilerParams(vmem_limit_bytes=nbytes(*chunks) + MARGIN),
        name="join",
    )(*chunks)


def on_device(
    donors, send_block, send_count, send_target, target_block, weights, halo_weights, permute
):
    block_rows = weights.shape[-1]
    rim_rows = halo_weights.shape[2] * block_rows
    count = lax.axis_size("dom")
    slabs = lax.axis_size("slab")
    far = list(range(count - 1, count // 2 - 1, -1))
    near = list(range(count // 2 - 1, 0, -1))
    tables = send_block[0, 0], send_count[0, 0], send_target[0, 0]
    places = target_block.shape[-1]
    form = functools.partial(form_parts, tables=tables, weights=weights[0, 0], places=places)
    *first, held = form(far, donors=donors, load=True, extra_rows=donors.shape[0])
    arrived = [send(part, step) for part, step in zip(first, far)]
    *second, rim = form(near + [0], donors=held, load=False, extra_rows=rim_rows)
    arrived += [send(part, step) for part, step in zip(second, near)] + [second[-1]]
    rim = lax.ppermute(rim, "slab", [(source, source + 1) for source in range(slabs - 1)])
    chosen, halo = prepare(permute[0, 0].reshape(-1, block_rows), halo_weights[0, 0], rim)
    steps = far + near + [0]
    chunks = place_parts(steps, count, target_block[0, 0].T, chosen, halo, arrived)
    final = [send(chunk, step) for chunk, step in zip(chunks, steps[:-1])] + [chunks[-1]]
    return join(steps, count, final)


def solution(mesh):
    return jax.shard_map(
        on_device,
        mesh=mesh,
        in_specs=(
            P(("slab", "dom"), None),
            P("slab", "dom", None, None),
            P("slab", "dom", None),
            P("slab", "dom", None, None),
            P("slab", "dom", None, None),
            P("slab", "dom", None, None, None, None),
            P("slab", "dom", None, None, None),
            P("slab", "dom", None),
        ),
        out_specs=P(("slab", "dom"), None),
        check_vma=False,
    )
```

```python
import functools

import jax
import jax.numpy as jnp
from jax import lax
from jax.experimental import pallas as pl
from jax.experimental.pallas import tpu as pltpu
from jax.sharding import PartitionSpec as P


VMEM = pl.BlockSpec(memory_space=pltpu.VMEM)
SMEM = pl.BlockSpec(memory_space=pltpu.SMEM)
HBM = pl.BlockSpec(memory_space=pltpu.HBM)
MARGIN = 4 << 20


def nbytes(*arrays):
    return sum(a.size * jnp.dtype(a.dtype).itemsize for a in arrays)


def swap(value, step):
    count = lax.axis_size("dom")
    return lax.ppermute(value, "dom", [(source, source ^ step) for source in range(count)])


def parts_kernel(steps, load, *refs):
    block_hbm, count_hbm, target_hbm, donors, weights = refs[:5]
    outs = refs[5 : 5 + len(steps)]
    extra = refs[5 + len(steps)]
    held_d = extra if load else donors
    block_of, count_of, target_of, held_w, sems, sem_w = refs[-6:]
    rows = held_w.shape[2]
    capacity = held_w.shape[1]
    width = held_d.shape[1]
    half = block_of.shape[0] // 2
    places = outs[0].shape[0] // (2 * rows)
    me = lax.axis_index("dom")
    owners = []
    for step in steps:
        owners += [jnp.bitwise_xor(me, step), jnp.bitwise_xor(me, step + half)]
    tables = [
        pltpu.make_async_copy(block_hbm, block_of, sems.at[0]),
        pltpu.make_async_copy(count_hbm, count_of, sems.at[1]),
        pltpu.make_async_copy(target_hbm, target_of, sems.at[2]),
    ]
    if load:
        tables.append(pltpu.make_async_copy(donors, held_d, sems.at[3]))
    loads = [
        pltpu.make_async_copy(weights.at[p], held_w.at[i], sem_w.at[i])
        for i, p in enumerate(owners)
    ]
    for copy in tables + loads:
        copy.start()
    for copy in tables:
        copy.wait()
    for i, p in enumerate(owners):
        loads[i].wait()
        total = None
        for c in range(0, capacity, 2):
            left = jnp.concatenate([held_w[i, c], held_w[i, c + 1]], axis=1)
            pieces = []
            for k in (c, c + 1):
                row = pl.multiple_of(block_of[p, k] * rows, rows)
                block = held_d[pl.ds(row, rows)]
                live = k < count_of[p]
                kept = []
                for t in range(places):
                    wanted = jnp.logical_and(live, target_of[p, k] == t)
                    kept.append(jnp.where(wanted, block, jnp.zeros_like(block)))
                pieces.append(jnp.concatenate(kept, axis=1))
            right = jnp.concatenate(pieces, axis=0)
            prod = jnp.dot(left, right, preferred_element_type=jnp.float32)
            total = prod if total is None else total + prod
        for t in range(places):
            at = ((i % 2) * places + t) * rows
            outs[i // 2][at : at + rows] = total[:, t * width : (t + 1) * width].astype(
                outs[0].dtype
            )
    if not load:
        extra[...] = held_d[held_d.shape[0] - extra.shape[0] : held_d.shape[0]]


def form_parts(steps, tables, donors, weights, places, load, extra_rows):
    _, capacity, rows, _ = weights.shape
    width = donors.shape[1]
    shapes = [jax.ShapeDtypeStruct((2 * places * rows, width), jnp.bfloat16)] * len(steps)
    shapes.append(jax.ShapeDtypeStruct((extra_rows, width), donors.dtype))
    in_hbm = functools.partial(pltpu.with_memory_space_constraint, memory_space=pltpu.HBM)
    held = jax.ShapeDtypeStruct((2 * len(steps), capacity, rows, rows), weights.dtype)
    return pl.pallas_call(
        functools.partial(parts_kernel, steps, load),
        out_shape=shapes,
        in_specs=[HBM, HBM, HBM, HBM if load else VMEM, HBM],
        out_specs=[VMEM] * len(shapes),
        scratch_shapes=[pltpu.SMEM(table.shape, table.dtype) for table in tables]
        + [
            pltpu.VMEM(held.shape, held.dtype),
            pltpu.SemaphoreType.DMA((4,)),
            pltpu.SemaphoreType.DMA((2 * len(steps),)),
        ],
        compiler_params=pltpu.CompilerParams(
            vmem_limit_bytes=nbytes(held, donors, *shapes) + MARGIN
        ),
        cost_estimate=pl.CostEstimate(
            flops=8 * len(steps) * capacity * rows * rows * width,
            bytes_accessed=nbytes(held, donors),
            transcendentals=0,
        ),
        name="parts",
    )(*map(in_hbm, tables), in_hbm(donors) if load else donors, in_hbm(weights))


def choose_kernel(steps, with_halo, place_of, order, *refs):
    halo_w = refs[0] if with_halo else None
    chosen = refs[-1]
    rows = order.shape[1]
    places = place_of.shape[0]
    me = lax.axis_index("dom")
    lane = lax.broadcasted_iota(jnp.int32, (rows, rows), 1)
    starts = []
    for step in steps:
        q = jnp.bitwise_xor(me, step)
        starts += [place_of[t, q] * rows for t in range(places)]

    def fill(j, carry):
        wanted = jnp.broadcast_to(order[pl.ds(j, 1), :], (rows, rows)).T - lane
        row = pl.multiple_of(j * rows, rows)
        for b, begin in enumerate(starts):
            chosen[pl.ds(row, rows), b * rows : (b + 1) * rows] = jnp.where(
                wanted == begin, 1.0, 0.0
            ).astype(jnp.bfloat16)
        if with_halo:
            first = jnp.where(wanted == 0, 1.0, 0.0).astype(jnp.bfloat16)
            for h in range(halo_w.shape[0]):
                at = (len(starts) + h) * rows
                chosen[pl.ds(row, rows), at : at + rows] = jnp.dot(
                    first, halo_w[h], preferred_element_type=jnp.float32
                ).astype(jnp.bfloat16)
        return carry

    lax.fori_loop(0, order.shape[0], fill, 0)


def choose(steps, place_of, order, halo_w=None):
    extra = [] if halo_w is None else [halo_w]
    columns = len(steps) * place_of.shape[0] * order.shape[1]
    columns += sum(h.shape[0] * h.shape[1] for h in extra)
    shape = jax.ShapeDtypeStruct((order.size, columns), jnp.bfloat16)
    return pl.pallas_call(
        functools.partial(choose_kernel, steps, bool(extra)),
        out_shape=shape,
        in_specs=[SMEM, VMEM] + [VMEM] * len(extra),
        out_specs=VMEM,
        compiler_params=pltpu.CompilerParams(
            vmem_limit_bytes=nbytes(order, shape, *extra) + MARGIN
        ),
        cost_estimate=pl.CostEstimate(
            flops=shape.size, bytes_accessed=nbytes(shape), transcendentals=0
        ),
        name="choose",
    )(place_of, order, *extra)


def place_kernel(steps, far, share, own, other, rim, *refs):
    outs = refs[-1 - len(steps) : -1]
    parts = refs[: -1 - len(steps)]
    rows_of = refs[-1]
    me = lax.axis_index("dom")
    lot = len(steps) * share
    half = len(steps)
    begin = jnp.bitwise_xor(me // half, 1 if far else 0) * lot
    begin = pl.multiple_of(begin, lot)
    depth = parts[0].shape[0] // 2
    for side, matrix in enumerate((own, other)):
        total = None
        for i, part in enumerate(parts):
            prod = jnp.dot(
                matrix[pl.ds(begin, lot), i * depth : (i + 1) * depth],
                part[side * depth : (side + 1) * depth],
                preferred_element_type=jnp.float32,
            )
            total = prod if total is None else total + prod
        if side == 0:
            total += jnp.dot(
                matrix[pl.ds(begin, lot), len(parts) * depth :],
                rim[...],
                preferred_element_type=jnp.float32,
            )
        rows_of[side] = total
    for step, out in zip(steps, outs):
        at = pl.multiple_of(lax.rem(jnp.bitwise_xor(me, step), half) * share, share)
        for side in range(2):
            out[side * share : (side + 1) * share] = rows_of[side, pl.ds(at, share)].astype(
                out.dtype
            )


def place(steps, far, share, own, other, rim, parts):
    width = rim.shape[1]
    shapes = [jax.ShapeDtypeStruct((2 * share, width), jnp.bfloat16)] * len(steps)
    held = jax.ShapeDtypeStruct((2, len(steps) * share, width), jnp.float32)
    return pl.pallas_call(
        functools.partial(place_kernel, steps, far, share),
        out_shape=shapes,
        in_specs=[VMEM] * (3 + len(parts)),
        out_specs=[VMEM] * len(shapes),
        scratch_shapes=[pltpu.VMEM(held.shape, held.dtype)],
        compiler_params=pltpu.CompilerParams(
            vmem_limit_bytes=nbytes(own, other, rim, held, *parts, *shapes) + MARGIN
        ),
        cost_estimate=pl.CostEstimate(
            flops=own.size * width * 2, bytes_accessed=nbytes(own), transcendentals=0
        ),
        name="place",
    )(own, other, rim, *parts)


def join_kernel(count, *refs):
    chunks = refs[:count]
    out, held, sem = refs[count:]
    share = chunks[0].shape[0] // 2
    me = lax.axis_index("dom")
    copies = []
    for step in range(count):
        row = pl.multiple_of(jnp.bitwise_xor(me, step) * share, share)
        pair = chunks[step ^ (count // 2)]
        total = chunks[step][:share].astype(jnp.float32) + pair[share:].astype(jnp.float32)
        held[step] = total.astype(held.dtype)
        copies.append(pltpu.make_async_copy(held.at[step], out.at[pl.ds(row, share)], sem.at[step]))
        copies[-1].start()
    for copy in copies:
        copy.wait()


def join(chunks):
    count = len(chunks)
    share, width = chunks[0].shape[0] // 2, chunks[0].shape[1]
    return pl.pallas_call(
        functools.partial(join_kernel, count),
        out_shape=jax.ShapeDtypeStruct((share * count, width), chunks[0].dtype),
        in_specs=[VMEM] * count,
        out_specs=HBM,
        scratch_shapes=[
            pltpu.VMEM((count, share, width), chunks[0].dtype),
            pltpu.SemaphoreType.DMA((count,)),
        ],
        compiler_params=pltpu.CompilerParams(vmem_limit_bytes=2 * nbytes(*chunks) + MARGIN),
        name="join",
    )(*chunks)


def on_device(
    donors, send_block, send_count, send_target, target_block, weights, halo_weights, permute
):
    block_rows = weights.shape[-1]
    rim_rows = halo_weights.shape[2] * block_rows
    count = lax.axis_size("dom")
    slabs = lax.axis_size("slab")
    half = count // 2
    share = permute.shape[-1] // count
    tables = send_block[0, 0], send_count[0, 0], send_target[0, 0]
    places = target_block.shape[-1]
    form = functools.partial(form_parts, tables=tables, weights=weights[0, 0], places=places)
    near = list(range(1, half))
    *first, held = form(near[:1], donors=donors, load=True, extra_rows=donors.shape[0])
    *second, rim = form(near[1:] + [0], donors=held, load=False, extra_rows=rim_rows)
    own_part = second.pop()
    arrived = [swap(part, step) for part, step in zip(first + second, near)]
    order = permute[0, 0].reshape(-1, block_rows)
    other_order = swap(order, half)
    table = target_block[0, 0].T
    other_table = swap(table, half)
    rim = lax.ppermute(rim, "slab", [(source, source + 1) for source in range(slabs - 1)])
    own = choose([0] + near, table, order, halo_weights[0, 0])
    other = choose([0] + near, other_table, other_order)
    parts = [own_part] + arrived
    far_steps = list(range(count - 1, half - 1, -1))
    far = place(far_steps, True, share, own, other, rim, parts)
    close_steps = list(range(half - 1, -1, -1))
    close = place(close_steps, False, share, own, other, rim, parts)
    chunks = [None] * count
    chunks[0] = close[-1]
    for step, chunk in zip(far_steps + close_steps[:-1], far + close[:-1]):
        chunks[step] = swap(chunk, step)
    return join(chunks)


def solution(mesh):
    return jax.shard_map(
        on_device,
        mesh=mesh,
        in_specs=(
            P(("slab", "dom"), None),
            P("slab", "dom", None, None),
            P("slab", "dom", None),
            P("slab", "dom", None, None),
            P("slab", "dom", None, None),
            P("slab", "dom", None, None, None, None),
            P("slab", "dom", None, None, None),
            P("slab", "dom", None),
        ),
        out_specs=P(("slab", "dom"), None),
        check_vma=False,
    )
```

```python
import functools

import jax
import jax.numpy as jnp
from jax import lax
from jax.experimental import pallas as pl
from jax.experimental.pallas import tpu as pltpu
from jax.sharding import PartitionSpec as P


VMEM = pl.BlockSpec(memory_space=pltpu.VMEM)
SMEM = pl.BlockSpec(memory_space=pltpu.SMEM)
HBM = pl.BlockSpec(memory_space=pltpu.HBM)
MARGIN = 4 << 20


def nbytes(*arrays):
    return sum(a.size * jnp.dtype(a.dtype).itemsize for a in arrays)


def swap(value, step):
    count = lax.axis_size("dom")
    return lax.ppermute(value, "dom", [(source, source ^ step) for source in range(count)])


def form_part(out, side, p, block_of, count_of, target_of, weight, block):
    capacity = block_of.shape[1]
    rows, width = weight(0).shape[0], out.shape[1]
    places = out.shape[0] // (2 * rows)
    total = None
    for c in range(0, capacity, 2):
        left = jnp.concatenate([weight(c), weight(c + 1)], axis=1)
        pieces = []
        for k in (c, c + 1):
            value = block(k)
            live = k < count_of[p]
            kept = []
            for t in range(places):
                wanted = jnp.logical_and(live, target_of[p, k] == t)
                kept.append(jnp.where(wanted, value, jnp.zeros_like(value)))
            pieces.append(jnp.concatenate(kept, axis=1))
        right = jnp.concatenate(pieces, axis=0)
        prod = jnp.dot(left, right, preferred_element_type=jnp.float32)
        total = prod if total is None else total + prod
    for t in range(places):
        at = (side * places + t) * rows
        out[at : at + rows] = total[:, t * width : (t + 1) * width].astype(out.dtype)


def owners_of(steps, half):
    me = lax.axis_index("dom")
    found = []
    for step in steps:
        found += [jnp.bitwise_xor(me, step), jnp.bitwise_xor(me, step + half)]
    return found


def gather_kernel(steps, block_hbm, count_hbm, target_hbm, donors, weights, *refs):
    outs = refs[: len(steps)]
    rim = refs[len(steps)]
    block_of, count_of, target_of, held_w, held_d, sems, sem_w, sem_d = refs[len(steps) + 1 :]
    capacity, rows = held_w.shape[1:3]
    owners = owners_of(steps, block_of.shape[0] // 2)
    tables = [
        pltpu.make_async_copy(block_hbm, block_of, sems.at[0]),
        pltpu.make_async_copy(count_hbm, count_of, sems.at[1]),
        pltpu.make_async_copy(target_hbm, target_of, sems.at[2]),
    ]
    tail = pltpu.make_async_copy(
        donors.at[pl.ds(donors.shape[0] - rim.shape[0], rim.shape[0])], rim, sems.at[3]
    )
    loads = [
        pltpu.make_async_copy(weights.at[p], held_w.at[i], sem_w.at[i])
        for i, p in enumerate(owners)
    ]
    for copy in tables + loads:
        copy.start()
    for copy in tables:
        copy.wait()
    for i, p in enumerate(owners):
        for c in range(capacity):
            row = pl.multiple_of(block_of[p, c] * rows, rows)
            copy = pltpu.make_async_copy(
                donors.at[pl.ds(row, rows)], held_d.at[i, c], sem_d.at[i, c]
            )
            copy.start()
            loads.append(copy)
    tail.start()
    for copy in loads:
        copy.wait()
    for i, p in enumerate(owners):
        form_part(
            outs[i // 2], i % 2, p, block_of, count_of, target_of,
            lambda c, i=i: held_w[i, c], lambda c, i=i: held_d[i, c],
        )
    tail.wait()


def part_shapes(steps, donors, weights, places):
    rows = 2 * places * weights.shape[2]
    return [jax.ShapeDtypeStruct((rows, donors.shape[1]), jnp.bfloat16)] * len(steps)


def gather_parts(steps, tables, donors, weights, places, rim_rows):
    capacity, rows = weights.shape[1:3]
    width = donors.shape[1]
    shapes = part_shapes(steps, donors, weights, places)
    shapes.append(jax.ShapeDtypeStruct((rim_rows, width), donors.dtype))
    in_hbm = functools.partial(pltpu.with_memory_space_constraint, memory_space=pltpu.HBM)
    held_w = jax.ShapeDtypeStruct((2 * len(steps), capacity, rows, rows), weights.dtype)
    held_d = jax.ShapeDtypeStruct((2 * len(steps), capacity, rows, width), donors.dtype)
    return pl.pallas_call(
        functools.partial(gather_kernel, steps),
        out_shape=shapes,
        in_specs=[HBM] * 5,
        out_specs=[VMEM] * len(shapes),
        scratch_shapes=[pltpu.SMEM(table.shape, table.dtype) for table in tables]
        + [
            pltpu.VMEM(held_w.shape, held_w.dtype),
            pltpu.VMEM(held_d.shape, held_d.dtype),
            pltpu.SemaphoreType.DMA((4,)),
            pltpu.SemaphoreType.DMA((2 * len(steps),)),
            pltpu.SemaphoreType.DMA((2 * len(steps), capacity)),
        ],
        compiler_params=pltpu.CompilerParams(
            vmem_limit_bytes=nbytes(held_w, held_d, *shapes) + MARGIN
        ),
        cost_estimate=pl.CostEstimate(
            flops=4 * held_w.size * width, bytes_accessed=nbytes(held_w), transcendentals=0
        ),
        name="gather",
    )(*map(in_hbm, [*tables, donors, weights]))


def parts_kernel(steps, block_of, count_of, target_of, donors, weights, *outs):
    rows = weights.shape[2]
    for i, p in enumerate(owners_of(steps, block_of.shape[0] // 2)):

        def block(c, p=p):
            row = pl.multiple_of(block_of[p, c] * rows, rows)
            return donors[pl.ds(row, rows)]

        form_part(
            outs[i // 2], i % 2, p, block_of, count_of, target_of,
            lambda c, p=p: weights[p, c], block,
        )


def form_parts(steps, tables, donors, weights, places):
    shapes = part_shapes(steps, donors, weights, places)
    return pl.pallas_call(
        functools.partial(parts_kernel, steps),
        out_shape=shapes,
        in_specs=[SMEM] * 3 + [VMEM] * 2,
        out_specs=[VMEM] * len(shapes),
        compiler_params=pltpu.CompilerParams(
            vmem_limit_bytes=nbytes(weights, donors, *shapes) + MARGIN
        ),
        cost_estimate=pl.CostEstimate(
            flops=4 * donors.size * len(steps),
            bytes_accessed=nbytes(weights),
            transcendentals=0,
        ),
        name="parts",
    )(*tables, donors, weights)


def choose_kernel(steps, with_halo, place_of, order, *refs):
    halo_w = refs[0] if with_halo else None
    chosen = refs[-1]
    rows = order.shape[1]
    places = place_of.shape[0]
    me = lax.axis_index("dom")
    lane = lax.broadcasted_iota(jnp.int32, (rows, rows), 1)
    starts = []
    for step in steps:
        q = jnp.bitwise_xor(me, step)
        starts += [place_of[t, q] * rows for t in range(places)]

    def fill(j, carry):
        wanted = (jnp.broadcast_to(order[pl.ds(j, 1), :], (rows, rows)).T - lane).astype(jnp.int16)
        row = pl.multiple_of(j * rows, rows)
        for b, begin in enumerate(starts):
            chosen[pl.ds(row, rows), b * rows : (b + 1) * rows] = jnp.where(
                wanted == begin.astype(jnp.int16), jnp.bfloat16(1), jnp.bfloat16(0)
            )
        if with_halo:
            first = jnp.where(wanted == 0, jnp.bfloat16(1), jnp.bfloat16(0))
            both = jnp.concatenate([halo_w[h] for h in range(halo_w.shape[0])], axis=1)
            chosen[pl.ds(row, rows), len(starts) * rows :] = jnp.dot(
                first, both, preferred_element_type=jnp.float32
            ).astype(jnp.bfloat16)
        return carry

    for j in range(order.shape[0]):
        fill(j, 0)


def choose(steps, place_of, order, halo_w=None):
    extra = [] if halo_w is None else [halo_w]
    columns = len(steps) * place_of.shape[0] * order.shape[1]
    columns += sum(h.shape[0] * h.shape[1] for h in extra)
    shape = jax.ShapeDtypeStruct((order.size, columns), jnp.bfloat16)
    return pl.pallas_call(
        functools.partial(choose_kernel, steps, bool(extra)),
        out_shape=shape,
        in_specs=[SMEM, VMEM] + [VMEM] * len(extra),
        out_specs=VMEM,
        compiler_params=pltpu.CompilerParams(
            vmem_limit_bytes=nbytes(order, shape, *extra) + MARGIN
        ),
        cost_estimate=pl.CostEstimate(
            flops=shape.size, bytes_accessed=nbytes(shape), transcendentals=0
        ),
        name="choose",
    )(place_of, order, *extra)


def place_kernel(steps, far, share, own, other, rim, *refs):
    outs = refs[-1 - len(steps) : -1]
    parts = refs[: -1 - len(steps)]
    rows_of = refs[-1]
    me = lax.axis_index("dom")
    lot = len(steps) * share
    half = len(steps)
    begin = jnp.bitwise_xor(me // half, 1 if far else 0) * lot
    begin = pl.multiple_of(begin, lot)
    depth = parts[0].shape[0] // 2
    for side, matrix in enumerate((own, other)):
        stack = [part[side * depth : (side + 1) * depth] for part in parts]
        if side == 0:
            stack.append(rim[...])
        total = jnp.dot(
            matrix[pl.ds(begin, lot)],
            jnp.concatenate(stack, axis=0),
            preferred_element_type=jnp.float32,
        )
        rows_of[side] = total
    for step, out in zip(steps, outs):
        at = pl.multiple_of(lax.rem(jnp.bitwise_xor(me, step), half) * share, share)
        for side in range(2):
            out[side * share : (side + 1) * share] = rows_of[side, pl.ds(at, share)].astype(
                out.dtype
            )


def place(steps, far, share, own, other, rim, parts):
    width = rim.shape[1]
    shapes = [jax.ShapeDtypeStruct((2 * share, width), jnp.bfloat16)] * len(steps)
    held = jax.ShapeDtypeStruct((2, len(steps) * share, width), jnp.float32)
    return pl.pallas_call(
        functools.partial(place_kernel, steps, far, share),
        out_shape=shapes,
        in_specs=[VMEM] * (3 + len(parts)),
        out_specs=[VMEM] * len(shapes),
        scratch_shapes=[pltpu.VMEM(held.shape, held.dtype)],
        compiler_params=pltpu.CompilerParams(
            vmem_limit_bytes=nbytes(own, other, rim, held, *parts, *shapes) + MARGIN
        ),
        cost_estimate=pl.CostEstimate(
            flops=own.size * width * 2, bytes_accessed=nbytes(own), transcendentals=0
        ),
        name="place",
    )(own, other, rim, *parts)


def join_kernel(count, *refs):
    chunks = refs[:count]
    out, held, sem = refs[count:]
    share = chunks[0].shape[0] // 2
    me = lax.axis_index("dom")
    copies = []
    for step in range(count):
        row = pl.multiple_of(jnp.bitwise_xor(me, step) * share, share)
        pair = chunks[step ^ (count // 2)]
        total = chunks[step][:share].astype(jnp.float32) + pair[share:].astype(jnp.float32)
        held[step] = total.astype(held.dtype)
        copies.append(pltpu.make_async_copy(held.at[step], out.at[pl.ds(row, share)], sem.at[step]))
        copies[-1].start()
    for copy in copies:
        copy.wait()


def join(chunks):
    count = len(chunks)
    share, width = chunks[0].shape[0] // 2, chunks[0].shape[1]
    return pl.pallas_call(
        functools.partial(join_kernel, count),
        out_shape=jax.ShapeDtypeStruct((share * count, width), chunks[0].dtype),
        in_specs=[VMEM] * count,
        out_specs=HBM,
        scratch_shapes=[
            pltpu.VMEM((count, share, width), chunks[0].dtype),
            pltpu.SemaphoreType.DMA((count,)),
        ],
        compiler_params=pltpu.CompilerParams(vmem_limit_bytes=2 * nbytes(*chunks) + MARGIN),
        name="join",
    )(*chunks)


def near_steps(count):
    half = count // 2
    return [half - 1] + list(range(1, half - 1))


def on_device(
    donors, send_block, send_count, send_target, target_block, weights, halo_weights, permute
):
    block_rows = weights.shape[-1]
    rim_rows = halo_weights.shape[2] * block_rows
    count = lax.axis_size("dom")
    slabs = lax.axis_size("slab")
    half = count // 2
    share = permute.shape[-1] // count
    tables = send_block[0, 0], send_count[0, 0], send_target[0, 0]
    places = target_block.shape[-1]
    near = near_steps(count)
    *first, rim = gather_parts(near[:1], tables, donors, weights[0, 0], places, rim_rows)
    second = form_parts(near[1:], tables, donors, weights[0, 0], places)
    third = form_parts([0], tables, donors, weights[0, 0], places)
    arrived = [swap(part, step) for part, step in zip([*first, *second], near)]
    order = permute[0, 0].reshape(-1, block_rows)
    other_order = swap(order, half)
    table = target_block[0, 0].T
    other_table = swap(table, half)
    rim = lax.ppermute(rim, "slab", [(source, source + 1) for source in range(slabs - 1)])
    own = choose([0] + near, table, order, halo_weights[0, 0])
    other = choose([0] + near, other_table, other_order)
    parts = [*third, *arrived]
    far_steps = list(range(count - 1, half - 1, -1))
    far = place(far_steps, True, share, own, other, rim, parts)
    close_steps = list(range(half - 1, -1, -1))
    close = place(close_steps, False, share, own, other, rim, parts)
    chunks = [None] * count
    chunks[0] = close[-1]
    for step, chunk in zip(far_steps + close_steps[:-1], far + close[:-1]):
        chunks[step] = swap(chunk, step)
    return join(chunks)


def solution(mesh):
    return jax.shard_map(
        on_device,
        mesh=mesh,
        in_specs=(
            P(("slab", "dom"), None),
            P("slab", "dom", None, None),
            P("slab", "dom", None),
            P("slab", "dom", None, None),
            P("slab", "dom", None, None),
            P("slab", "dom", None, None, None, None),
            P("slab", "dom", None, None, None),
            P("slab", "dom", None),
        ),
        out_specs=P(("slab", "dom"), None),
        check_vma=False,
    )
```

```python
import functools

import jax
import jax.numpy as jnp
from jax import lax
from jax.experimental import pallas as pl
from jax.experimental.pallas import tpu as pltpu
from jax.sharding import PartitionSpec as P


VMEM = pl.BlockSpec(memory_space=pltpu.VMEM)
SMEM = pl.BlockSpec(memory_space=pltpu.SMEM)
HBM = pl.BlockSpec(memory_space=pltpu.HBM)
MARGIN = 4 << 20


def nbytes(*arrays):
    return sum(a.size * jnp.dtype(a.dtype).itemsize for a in arrays)


def swap(value, step):
    count = lax.axis_size("dom")
    return lax.ppermute(value, "dom", [(source, source ^ step) for source in range(count)])


def form_part(out, side, p, block_of, count_of, target_of, weight, block):
    capacity = block_of.shape[1]
    rows, width = weight(0).shape[0], out.shape[1]
    places = out.shape[0] // (2 * rows)
    pieces = []
    for k in range(capacity):
        value = block(k)
        live = k < count_of[p]
        kept = []
        for t in range(places):
            wanted = jnp.logical_and(live, target_of[p, k] == t)
            kept.append(jnp.where(wanted, value, jnp.zeros_like(value)))
        pieces.append(jnp.concatenate(kept, axis=1))
    total = jnp.dot(
        jnp.concatenate([weight(k) for k in range(capacity)], axis=1),
        jnp.concatenate(pieces, axis=0),
        preferred_element_type=jnp.float32,
    )
    for t in range(places):
        at = (side * places + t) * rows
        out[at : at + rows] = total[:, t * width : (t + 1) * width].astype(out.dtype)


def parts_kernel(steps, tables_hbm, order_hbm, table_hbm, donors, weights, *refs):
    outs = refs[: len(steps)]
    rim, packed = refs[len(steps) : len(steps) + 2]
    block_of, count_of, target_of, held_t, held_w, held_d, sems, sem_w = refs[len(steps) + 2 :]
    rows = held_w.shape[2]
    half = block_of.shape[0] // 2
    me = lax.axis_index("dom")
    owners = [(jnp.bitwise_xor(me, step), jnp.bitwise_xor(me, step + half)) for step in steps]
    copies = [
        pltpu.make_async_copy(source, target, sems.at[i])
        for i, (source, target) in enumerate(
            [
                *zip(tables_hbm, (block_of, count_of, target_of)),
                (donors, held_d),
                (order_hbm, packed.at[0 : order_hbm.shape[0]]),
                (table_hbm, held_t),
            ]
        )
    ]
    loads = [
        [
            pltpu.make_async_copy(weights.at[p], held_w.at[2 * i + j], sem_w.at[2 * i + j])
            for j, p in enumerate(pair)
        ]
        for i, pair in enumerate(owners)
    ]
    for copy in copies[:4] + sum(loads, []) + copies[4:]:
        copy.start()
    for copy in copies[:4] + sum(loads, []):
        copy.wait()
    for i, pair in enumerate(owners):
        for j, p in enumerate(pair):

            def block(c, p=p):
                row = pl.multiple_of(block_of[p, c] * rows, rows)
                return held_d[pl.ds(row, rows)]

            form_part(
                outs[i], j, p, block_of, count_of, target_of,
                lambda c, at=2 * i + j: held_w[at, c], block,
            )
    rim[...] = held_d[held_d.shape[0] - rim.shape[0] : held_d.shape[0]]
    for copy in copies[4:]:
        copy.wait()
    packed[order_hbm.shape[0] : order_hbm.shape[0] + held_t.shape[0], 0 : held_t.shape[1]] = (
        held_t[...]
    )


def form_parts(steps, tables, order, table, donors, weights, rim_rows):
    rows, width = weights.shape[2], donors.shape[1]
    places = table.shape[0]
    shapes = [jax.ShapeDtypeStruct((2 * places * rows, width), jnp.bfloat16)] * len(steps)
    shapes += [
        jax.ShapeDtypeStruct((rim_rows, width), donors.dtype),
        jax.ShapeDtypeStruct((order.shape[0] + 8, order.shape[1]), order.dtype),
    ]
    in_hbm = functools.partial(pltpu.with_memory_space_constraint, memory_space=pltpu.HBM)

    def kernel(block_hbm, count_hbm, target_hbm, *refs):
        parts_kernel(steps, (block_hbm, count_hbm, target_hbm), *refs)

    return pl.pallas_call(
        kernel,
        out_shape=shapes,
        in_specs=[HBM] * 7,
        out_specs=[VMEM] * len(shapes),
        scratch_shapes=[pltpu.SMEM(item.shape, item.dtype) for item in tables]
        + [
            pltpu.VMEM(table.shape, table.dtype),
            pltpu.VMEM(weights.shape, weights.dtype),
            pltpu.VMEM(donors.shape, donors.dtype),
            pltpu.SemaphoreType.DMA((6,)),
            pltpu.SemaphoreType.DMA((2 * len(steps),)),
        ],
        compiler_params=pltpu.CompilerParams(
            vmem_limit_bytes=nbytes(weights, donors, *shapes) + MARGIN
        ),
        cost_estimate=pl.CostEstimate(
            flops=4 * weights.size * width,
            bytes_accessed=nbytes(weights, donors),
            transcendentals=0,
        ),
        name="parts",
    )(*map(in_hbm, [*tables, order, table, donors, weights]))


def choose_kernel(steps, with_halo, places, packed, *refs):
    halo_w = refs[0] if with_halo else None
    chosen, place_of, sem = refs[-3:]
    blocks, rows = packed.shape[0] - place_of.shape[0], packed.shape[1]
    copy = pltpu.make_async_copy(packed.at[pl.ds(blocks, place_of.shape[0])], place_of, sem)
    copy.start()
    copy.wait()
    me = lax.axis_index("dom")
    lane = lax.broadcasted_iota(jnp.int32, (rows, rows), 1)
    starts = []
    for step in steps:
        q = jnp.bitwise_xor(me, step)
        starts += [place_of[t, q] * rows for t in range(places)]

    def fill(j, carry):
        wanted = (jnp.broadcast_to(packed[pl.ds(j, 1), :], (rows, rows)).T - lane).astype(jnp.int16)
        row = pl.multiple_of(j * rows, rows)
        for b, begin in enumerate(starts):
            chosen[pl.ds(row, rows), b * rows : (b + 1) * rows] = jnp.where(
                wanted == begin.astype(jnp.int16), jnp.bfloat16(1), jnp.bfloat16(0)
            )
        if with_halo:
            first = jnp.where(wanted == 0, jnp.bfloat16(1), jnp.bfloat16(0))
            both = jnp.concatenate([halo_w[h] for h in range(halo_w.shape[0])], axis=1)
            chosen[pl.ds(row, rows), len(starts) * rows :] = jnp.dot(
                first, both, preferred_element_type=jnp.float32
            ).astype(jnp.bfloat16)
        return carry

    for j in range(blocks):
        fill(j, 0)


def choose(steps, places, packed, halo_w=None):
    extra = [] if halo_w is None else [halo_w]
    blocks, rows = packed.shape[0] - 8, packed.shape[1]
    columns = len(steps) * places * rows + sum(h.shape[0] * h.shape[1] for h in extra)
    shape = jax.ShapeDtypeStruct((blocks * rows, columns), jnp.bfloat16)
    return pl.pallas_call(
        functools.partial(choose_kernel, steps, bool(extra), places),
        out_shape=shape,
        in_specs=[VMEM] * (1 + len(extra)),
        out_specs=VMEM,
        scratch_shapes=[pltpu.SMEM((8, rows), packed.dtype), pltpu.SemaphoreType.DMA(())],
        compiler_params=pltpu.CompilerParams(
            vmem_limit_bytes=nbytes(packed, shape, *extra) + MARGIN
        ),
        cost_estimate=pl.CostEstimate(
            flops=shape.size, bytes_accessed=nbytes(shape), transcendentals=0
        ),
        name="choose",
    )(packed, *extra)


def place_kernel(steps, far, share, own, other, rim, *refs):
    outs = refs[-1 - len(steps) : -1]
    parts = refs[: -1 - len(steps)]
    rows_of = refs[-1]
    me = lax.axis_index("dom")
    lot = len(steps) * share
    half = len(steps)
    begin = jnp.bitwise_xor(me // half, 1 if far else 0) * lot
    begin = pl.multiple_of(begin, lot)
    depth = parts[0].shape[0] // 2
    for side, matrix in enumerate((own, other)):
        stack = [part[side * depth : (side + 1) * depth] for part in parts]
        if side == 0:
            stack.append(rim[...])
        total = jnp.dot(
            matrix[pl.ds(begin, lot)],
            jnp.concatenate(stack, axis=0),
            preferred_element_type=jnp.float32,
        )
        rows_of[side] = total
    for step, out in zip(steps, outs):
        at = pl.multiple_of(lax.rem(jnp.bitwise_xor(me, step), half) * share, share)
        for side in range(2):
            out[side * share : (side + 1) * share] = rows_of[side, pl.ds(at, share)].astype(
                out.dtype
            )


def place(steps, far, share, own, other, rim, parts):
    width = rim.shape[1]
    shapes = [jax.ShapeDtypeStruct((2 * share, width), jnp.bfloat16)] * len(steps)
    held = jax.ShapeDtypeStruct((2, len(steps) * share, width), jnp.float32)
    return pl.pallas_call(
        functools.partial(place_kernel, steps, far, share),
        out_shape=shapes,
        in_specs=[VMEM] * (3 + len(parts)),
        out_specs=[VMEM] * len(shapes),
        scratch_shapes=[pltpu.VMEM(held.shape, held.dtype)],
        compiler_params=pltpu.CompilerParams(
            vmem_limit_bytes=nbytes(own, other, rim, held, *parts, *shapes) + MARGIN
        ),
        cost_estimate=pl.CostEstimate(
            flops=own.size * width * 2, bytes_accessed=nbytes(own), transcendentals=0
        ),
        name="place",
    )(own, other, rim, *parts)


def join_kernel(count, *refs):
    chunks = refs[:count]
    out, held, sem = refs[count:]
    share = chunks[0].shape[0] // 2
    me = lax.axis_index("dom")
    copies = []
    for step in range(count):
        row = pl.multiple_of(jnp.bitwise_xor(me, step) * share, share)
        pair = chunks[step ^ (count // 2)]
        total = chunks[step][:share].astype(jnp.float32) + pair[share:].astype(jnp.float32)
        held[step] = total.astype(held.dtype)
        copies.append(pltpu.make_async_copy(held.at[step], out.at[pl.ds(row, share)], sem.at[step]))
        copies[-1].start()
    for copy in copies:
        copy.wait()


def join(chunks):
    count = len(chunks)
    share, width = chunks[0].shape[0] // 2, chunks[0].shape[1]
    return pl.pallas_call(
        functools.partial(join_kernel, count),
        out_shape=jax.ShapeDtypeStruct((share * count, width), chunks[0].dtype),
        in_specs=[VMEM] * count,
        out_specs=HBM,
        scratch_shapes=[
            pltpu.VMEM((count, share, width), chunks[0].dtype),
            pltpu.SemaphoreType.DMA((count,)),
        ],
        compiler_params=pltpu.CompilerParams(vmem_limit_bytes=2 * nbytes(*chunks) + MARGIN),
        name="join",
    )(*chunks)


def near_steps(count):
    half = count // 2
    return list(range(1, half))


def on_device(
    donors, send_block, send_count, send_target, target_block, weights, halo_weights, permute
):
    block_rows = weights.shape[-1]
    rim_rows = halo_weights.shape[2] * block_rows
    count = lax.axis_size("dom")
    slabs = lax.axis_size("slab")
    half = count // 2
    share = permute.shape[-1] // count
    tables = send_block[0, 0], send_count[0, 0], send_target[0, 0]
    places = target_block.shape[-1]
    near = near_steps(count)
    order = permute[0, 0].reshape(-1, block_rows)
    *formed, own_part, rim, packed = form_parts(
        near + [0], tables, order, target_block[0, 0].T, donors, weights[0, 0], rim_rows
    )
    arrived = [swap(part, step) for part, step in zip(formed, near)]
    other_packed = swap(packed, half)
    rim = lax.ppermute(rim, "slab", [(source, source + 1) for source in range(slabs - 1)])
    own = choose([0] + near, places, packed, halo_weights[0, 0])
    other = choose([0] + near, places, other_packed)
    parts = [own_part, *arrived]
    far_steps = list(range(half, count))
    far = place(far_steps, True, share, own, other, rim, parts)
    close_steps = list(range(1, half)) + [0]
    close = place(close_steps, False, share, own, other, rim, parts)
    chunks = [None] * count
    chunks[0] = close[-1]
    for step, chunk in zip(far_steps + close_steps[:-1], far + close[:-1]):
        chunks[step] = swap(chunk, step)
    return join(chunks)


def solution(mesh):
    return jax.shard_map(
        on_device,
        mesh=mesh,
        in_specs=(
            P(("slab", "dom"), None),
            P("slab", "dom", None, None),
            P("slab", "dom", None),
            P("slab", "dom", None, None),
            P("slab", "dom", None, None),
            P("slab", "dom", None, None, None, None),
            P("slab", "dom", None, None, None),
            P("slab", "dom", None),
        ),
        out_specs=P(("slab", "dom"), None),
        check_vma=False,
    )
```

```python
import functools

import jax
import jax.numpy as jnp
from jax import lax
from jax.experimental import pallas as pl
from jax.experimental.pallas import tpu as pltpu
from jax.sharding import PartitionSpec as P


VMEM = pl.BlockSpec(memory_space=pltpu.VMEM)
SMEM = pl.BlockSpec(memory_space=pltpu.SMEM)
HBM = pl.BlockSpec(memory_space=pltpu.HBM)
MARGIN = 4 << 20


def nbytes(*arrays):
    return sum(a.size * jnp.dtype(a.dtype).itemsize for a in arrays)


def swap(value, step):
    count = lax.axis_size("dom")
    return lax.ppermute(value, "dom", [(source, source ^ step) for source in range(count)])


def form_part(out, side, p, block_of, count_of, target_of, weight, block):
    capacity = block_of.shape[1]
    rows, width = weight(0).shape[0], out.shape[1]
    places = out.shape[0] // (2 * rows)
    pieces = []
    for k in range(capacity):
        value = block(k)
        live = k < count_of[p]
        kept = []
        for t in range(places):
            wanted = jnp.logical_and(live, target_of[p, k] == t)
            kept.append(jnp.where(wanted, value, jnp.zeros_like(value)))
        pieces.append(jnp.concatenate(kept, axis=1))
    total = jnp.dot(
        jnp.concatenate([weight(k) for k in range(capacity)], axis=1),
        jnp.concatenate(pieces, axis=0),
        preferred_element_type=jnp.float32,
    )
    for t in range(places):
        at = (side * places + t) * rows
        out[at : at + rows] = total[:, t * width : (t + 1) * width].astype(out.dtype)


def parts_kernel(steps, tables_hbm, order_hbm, table_hbm, donors, weights, *refs):
    outs = refs[: len(steps)]
    rim, packed = refs[len(steps) : len(steps) + 2]
    block_of, count_of, target_of, held_t, held_w, held_d, sems, sem_w = refs[len(steps) + 2 :]
    rows = held_w.shape[2]
    half = block_of.shape[0] // 2
    me = lax.axis_index("dom")
    owners = [(jnp.bitwise_xor(me, step), jnp.bitwise_xor(me, step + half)) for step in steps]
    copies = [
        pltpu.make_async_copy(source, target, sems.at[i])
        for i, (source, target) in enumerate(
            [
                *zip(tables_hbm, (block_of, count_of, target_of)),
                (donors, held_d),
                (order_hbm, packed.at[0 : order_hbm.shape[0]]),
                (table_hbm, held_t),
            ]
        )
    ]
    loads = [
        [
            pltpu.make_async_copy(weights.at[p], held_w.at[2 * i + j], sem_w.at[2 * i + j])
            for j, p in enumerate(pair)
        ]
        for i, pair in enumerate(owners)
    ]
    for copy in copies[:4] + sum(loads, []) + copies[4:]:
        copy.start()
    for copy in copies[:4] + sum(loads, []):
        copy.wait()
    for i, pair in enumerate(owners):
        for j, p in enumerate(pair):

            def block(c, p=p):
                row = pl.multiple_of(block_of[p, c] * rows, rows)
                return held_d[pl.ds(row, rows)]

            form_part(
                outs[i], j, p, block_of, count_of, target_of,
                lambda c, at=2 * i + j: held_w[at, c], block,
            )
    rim[...] = held_d[held_d.shape[0] - rim.shape[0] : held_d.shape[0]]
    for copy in copies[4:]:
        copy.wait()
    packed[order_hbm.shape[0] : order_hbm.shape[0] + held_t.shape[0], 0 : held_t.shape[1]] = (
        held_t[...]
    )


def form_parts(steps, tables, order, table, donors, weights, rim_rows):
    rows, width = weights.shape[2], donors.shape[1]
    places = table.shape[0]
    shapes = [jax.ShapeDtypeStruct((2 * places * rows, width), jnp.bfloat16)] * len(steps)
    shapes += [
        jax.ShapeDtypeStruct((rim_rows, width), donors.dtype),
        jax.ShapeDtypeStruct((order.shape[0] + 8, order.shape[1]), order.dtype),
    ]
    in_hbm = functools.partial(pltpu.with_memory_space_constraint, memory_space=pltpu.HBM)

    def kernel(block_hbm, count_hbm, target_hbm, *refs):
        parts_kernel(steps, (block_hbm, count_hbm, target_hbm), *refs)

    return pl.pallas_call(
        kernel,
        out_shape=shapes,
        in_specs=[HBM] * 7,
        out_specs=[VMEM] * len(shapes),
        scratch_shapes=[pltpu.SMEM(item.shape, item.dtype) for item in tables]
        + [
            pltpu.VMEM(table.shape, table.dtype),
            pltpu.VMEM(weights.shape, weights.dtype),
            pltpu.VMEM(donors.shape, donors.dtype),
            pltpu.SemaphoreType.DMA((6,)),
            pltpu.SemaphoreType.DMA((2 * len(steps),)),
        ],
        compiler_params=pltpu.CompilerParams(
            vmem_limit_bytes=nbytes(weights, donors, *shapes) + MARGIN
        ),
        cost_estimate=pl.CostEstimate(
            flops=4 * weights.size * width,
            bytes_accessed=nbytes(weights, donors),
            transcendentals=0,
        ),
        name="parts",
    )(*map(in_hbm, [*tables, order, table, donors, weights]))


def choose_kernel(steps, with_halo, places, packed, *refs):
    halo_w = refs[0] if with_halo else None
    chosen = refs[-1]
    blocks, rows = packed.shape[0] - 8, packed.shape[1]
    column = lax.broadcasted_iota(jnp.int32, (1, rows), 1)
    me = lax.axis_index("dom")
    lane = lax.broadcasted_iota(jnp.int32, (rows, rows), 1)
    starts = []
    for step in steps:
        q = jnp.bitwise_xor(me, step)
        for t in range(places):
            table = packed[blocks + t : blocks + t + 1]
            place = jnp.sum(jnp.where(column == q, table, 0), axis=1, keepdims=True)
            starts.append(jnp.broadcast_to(place * rows, (rows, rows)).astype(jnp.int16))

    def fill(j, carry):
        wanted = (jnp.broadcast_to(packed[pl.ds(j, 1), :], (rows, rows)).T - lane).astype(jnp.int16)
        row = pl.multiple_of(j * rows, rows)
        for b, begin in enumerate(starts):
            chosen[pl.ds(row, rows), b * rows : (b + 1) * rows] = jnp.where(
                wanted == begin, jnp.bfloat16(1), jnp.bfloat16(0)
            )
        if with_halo:
            first = jnp.where(wanted == 0, jnp.bfloat16(1), jnp.bfloat16(0))
            both = jnp.concatenate([halo_w[h] for h in range(halo_w.shape[0])], axis=1)
            chosen[pl.ds(row, rows), len(starts) * rows :] = jnp.dot(
                first, both, preferred_element_type=jnp.float32
            ).astype(jnp.bfloat16)
        return carry

    for j in range(blocks):
        fill(j, 0)


def choose(steps, places, packed, halo_w=None):
    extra = [] if halo_w is None else [halo_w]
    blocks, rows = packed.shape[0] - 8, packed.shape[1]
    columns = len(steps) * places * rows + sum(h.shape[0] * h.shape[1] for h in extra)
    shape = jax.ShapeDtypeStruct((blocks * rows, columns), jnp.bfloat16)
    return pl.pallas_call(
        functools.partial(choose_kernel, steps, bool(extra), places),
        out_shape=shape,
        in_specs=[VMEM] * (1 + len(extra)),
        out_specs=VMEM,
        compiler_params=pltpu.CompilerParams(
            vmem_limit_bytes=nbytes(packed, shape, *extra) + MARGIN
        ),
        cost_estimate=pl.CostEstimate(
            flops=shape.size, bytes_accessed=nbytes(shape), transcendentals=0
        ),
        name="choose",
    )(packed, *extra)


def place_kernel(steps, far, share, own, other, rim, *refs):
    outs = refs[-1 - len(steps) : -1]
    parts = refs[: -1 - len(steps)]
    rows_of = refs[-1]
    me = lax.axis_index("dom")
    lot = len(steps) * share
    half = len(steps)
    begin = jnp.bitwise_xor(me // half, 1 if far else 0) * lot
    begin = pl.multiple_of(begin, lot)
    depth = parts[0].shape[0] // 2
    for side, matrix in enumerate((own, other)):
        stack = [part[side * depth : (side + 1) * depth] for part in parts]
        if side == 0:
            stack.append(rim[...])
        total = jnp.dot(
            matrix[pl.ds(begin, lot)],
            jnp.concatenate(stack, axis=0),
            preferred_element_type=jnp.float32,
        )
        rows_of[side] = total
    for step, out in zip(steps, outs):
        at = pl.multiple_of(lax.rem(jnp.bitwise_xor(me, step), half) * share, share)
        for side in range(2):
            out[side * share : (side + 1) * share] = rows_of[side, pl.ds(at, share)].astype(
                out.dtype
            )


def place(steps, far, share, own, other, rim, parts):
    width = rim.shape[1]
    shapes = [jax.ShapeDtypeStruct((2 * share, width), jnp.bfloat16)] * len(steps)
    held = jax.ShapeDtypeStruct((2, len(steps) * share, width), jnp.float32)
    return pl.pallas_call(
        functools.partial(place_kernel, steps, far, share),
        out_shape=shapes,
        in_specs=[VMEM] * (3 + len(parts)),
        out_specs=[VMEM] * len(shapes),
        scratch_shapes=[pltpu.VMEM(held.shape, held.dtype)],
        compiler_params=pltpu.CompilerParams(
            vmem_limit_bytes=nbytes(own, other, rim, held, *parts, *shapes) + MARGIN
        ),
        cost_estimate=pl.CostEstimate(
            flops=own.size * width * 2, bytes_accessed=nbytes(own), transcendentals=0
        ),
        name="place",
    )(own, other, rim, *parts)


def join_kernel(count, *refs):
    chunks = refs[:count]
    out, held, sem = refs[count:]
    share = chunks[0].shape[0] // 2
    me = lax.axis_index("dom")
    copies = []
    for step in range(count):
        row = pl.multiple_of(jnp.bitwise_xor(me, step) * share, share)
        pair = chunks[step ^ (count // 2)]
        total = chunks[step][:share].astype(jnp.float32) + pair[share:].astype(jnp.float32)
        held[step] = total.astype(held.dtype)
        copies.append(pltpu.make_async_copy(held.at[step], out.at[pl.ds(row, share)], sem.at[step]))
        copies[-1].start()
    for copy in copies:
        copy.wait()


def join(chunks):
    count = len(chunks)
    share, width = chunks[0].shape[0] // 2, chunks[0].shape[1]
    return pl.pallas_call(
        functools.partial(join_kernel, count),
        out_shape=jax.ShapeDtypeStruct((share * count, width), chunks[0].dtype),
        in_specs=[VMEM] * count,
        out_specs=HBM,
        scratch_shapes=[
            pltpu.VMEM((count, share, width), chunks[0].dtype),
            pltpu.SemaphoreType.DMA((count,)),
        ],
        compiler_params=pltpu.CompilerParams(vmem_limit_bytes=2 * nbytes(*chunks) + MARGIN),
        name="join",
    )(*chunks)


def near_steps(count):
    half = count // 2
    return list(range(1, half))


def on_device(
    donors, send_block, send_count, send_target, target_block, weights, halo_weights, permute
):
    block_rows = weights.shape[-1]
    rim_rows = halo_weights.shape[2] * block_rows
    count = lax.axis_size("dom")
    slabs = lax.axis_size("slab")
    half = count // 2
    share = permute.shape[-1] // count
    tables = send_block[0, 0], send_count[0, 0], send_target[0, 0]
    places = target_block.shape[-1]
    near = near_steps(count)
    order = permute[0, 0].reshape(-1, block_rows)
    *formed, own_part, rim, packed = form_parts(
        near + [0], tables, order, target_block[0, 0].T, donors, weights[0, 0], rim_rows
    )
    arrived = [swap(part, step) for part, step in zip(formed, near)]
    other_packed = swap(packed, half)
    rim = lax.ppermute(rim, "slab", [(source, source + 1) for source in range(slabs - 1)])
    own = choose([0] + near, places, packed, halo_weights[0, 0])
    other = choose([0] + near, places, other_packed)
    parts = [own_part, *arrived]
    far_steps = list(range(half, count))
    far = place(far_steps, True, share, own, other, rim, parts)
    close_steps = list(range(1, half)) + [0]
    close = place(close_steps, False, share, own, other, rim, parts)
    chunks = [None] * count
    chunks[0] = close[-1]
    for step, chunk in zip(far_steps + close_steps[:-1], far + close[:-1]):
        chunks[step] = swap(chunk, step)
    return join(chunks)


def solution(mesh):
    return jax.shard_map(
        on_device,
        mesh=mesh,
        in_specs=(
            P(("slab", "dom"), None),
            P("slab", "dom", None, None),
            P("slab", "dom", None),
            P("slab", "dom", None, None),
            P("slab", "dom", None, None),
            P("slab", "dom", None, None, None, None),
            P("slab", "dom", None, None, None),
            P("slab", "dom", None),
        ),
        out_specs=P(("slab", "dom"), None),
        check_vma=False,
    )
```

```python
import functools

import jax
import jax.numpy as jnp
from jax import lax
from jax.experimental import pallas as pl
from jax.experimental.pallas import tpu as pltpu
from jax.sharding import PartitionSpec as P


VMEM = pl.BlockSpec(memory_space=pltpu.VMEM)
SMEM = pl.BlockSpec(memory_space=pltpu.SMEM)
HBM = pl.BlockSpec(memory_space=pltpu.HBM)
MARGIN = 4 << 20


def nbytes(*arrays):
    return sum(a.size * jnp.dtype(a.dtype).itemsize for a in arrays)


def swap(value, step):
    count = lax.axis_size("dom")
    return lax.ppermute(value, "dom", [(source, source ^ step) for source in range(count)])


def form_part(out, side, p, block_of, count_of, target_of, weight, block):
    capacity = block_of.shape[1]
    rows, width = weight(0).shape[0], out.shape[1]
    places = out.shape[0] // (2 * rows)
    pieces = []
    for k in range(capacity):
        value = block(k)
        live = k < count_of[p]
        kept = []
        for t in range(places):
            wanted = jnp.logical_and(live, target_of[p, k] == t)
            kept.append(jnp.where(wanted, value, jnp.zeros_like(value)))
        pieces.append(jnp.concatenate(kept, axis=1))
    total = jnp.dot(
        jnp.concatenate([weight(k) for k in range(capacity)], axis=1),
        jnp.concatenate(pieces, axis=0),
        preferred_element_type=jnp.float32,
    )
    for t in range(places):
        at = (side * places + t) * rows
        out[at : at + rows] = total[:, t * width : (t + 1) * width].astype(out.dtype)


def parts_kernel(steps, tables_hbm, order_hbm, table_hbm, donors, weights, *refs):
    outs = refs[: len(steps)]
    rim, packed = refs[len(steps) : len(steps) + 2]
    block_of, count_of, target_of, held_t, held_w, held_d, sems, sem_w = refs[len(steps) + 2 :]
    rows = held_w.shape[2]
    half = block_of.shape[0] // 2
    me = lax.axis_index("dom")
    owners = [(jnp.bitwise_xor(me, step), jnp.bitwise_xor(me, step + half)) for step in steps]
    copies = [
        pltpu.make_async_copy(source, target, sems.at[i])
        for i, (source, target) in enumerate(
            [
                *zip(tables_hbm, (block_of, count_of, target_of)),
                (donors, held_d),
                (order_hbm, packed.at[0 : order_hbm.shape[0]]),
                (table_hbm, held_t),
            ]
        )
    ]
    loads = [
        [
            pltpu.make_async_copy(weights.at[p], held_w.at[2 * i + j], sem_w.at[2 * i + j])
            for j, p in enumerate(pair)
        ]
        for i, pair in enumerate(owners)
    ]
    for copy in copies[:4] + sum(loads, []) + copies[4:]:
        copy.start()
    for copy in copies[:4] + sum(loads, []):
        copy.wait()
    for i, pair in enumerate(owners):
        for j, p in enumerate(pair):

            def block(c, p=p):
                row = pl.multiple_of(block_of[p, c] * rows, rows)
                return held_d[pl.ds(row, rows)]

            form_part(
                outs[i], j, p, block_of, count_of, target_of,
                lambda c, at=2 * i + j: held_w[at, c], block,
            )
    rim[...] = held_d[held_d.shape[0] - rim.shape[0] : held_d.shape[0]]
    for copy in copies[4:]:
        copy.wait()
    packed[order_hbm.shape[0] : order_hbm.shape[0] + held_t.shape[0], 0 : held_t.shape[1]] = (
        held_t[...]
    )


def form_parts(steps, tables, order, table, donors, weights, rim_rows):
    rows, width = weights.shape[2], donors.shape[1]
    places = table.shape[0]
    shapes = [jax.ShapeDtypeStruct((2 * places * rows, width), jnp.bfloat16)] * len(steps)
    shapes += [
        jax.ShapeDtypeStruct((rim_rows, width), donors.dtype),
        jax.ShapeDtypeStruct((order.shape[0] + 8, order.shape[1]), order.dtype),
    ]
    in_hbm = functools.partial(pltpu.with_memory_space_constraint, memory_space=pltpu.HBM)

    def kernel(block_hbm, count_hbm, target_hbm, *refs):
        parts_kernel(steps, (block_hbm, count_hbm, target_hbm), *refs)

    return pl.pallas_call(
        kernel,
        out_shape=shapes,
        in_specs=[HBM] * 7,
        out_specs=[VMEM] * len(shapes),
        scratch_shapes=[pltpu.SMEM(item.shape, item.dtype) for item in tables]
        + [
            pltpu.VMEM(table.shape, table.dtype),
            pltpu.VMEM(weights.shape, weights.dtype),
            pltpu.VMEM(donors.shape, donors.dtype),
            pltpu.SemaphoreType.DMA((6,)),
            pltpu.SemaphoreType.DMA((2 * len(steps),)),
        ],
        compiler_params=pltpu.CompilerParams(
            vmem_limit_bytes=nbytes(weights, donors, *shapes) + MARGIN
        ),
        cost_estimate=pl.CostEstimate(
            flops=4 * weights.size * width,
            bytes_accessed=nbytes(weights, donors),
            transcendentals=0,
        ),
        name="parts",
    )(*map(in_hbm, [*tables, order, table, donors, weights]))


def choose_kernel(steps, with_halo, places, packed, *refs):
    halo_w = refs[0] if with_halo else None
    chosen = refs[-1]
    blocks, rows = packed.shape[0] - 8, packed.shape[1]
    column = lax.broadcasted_iota(jnp.int32, (1, rows), 1)
    me = lax.axis_index("dom")
    lane = lax.broadcasted_iota(jnp.int32, (rows, rows), 1)
    starts = []
    for step in steps:
        q = jnp.bitwise_xor(me, step)
        for t in range(places):
            table = packed[blocks + t : blocks + t + 1]
            place = jnp.sum(jnp.where(column == q, table, 0), axis=1, keepdims=True)
            starts.append(jnp.broadcast_to(place * rows, (rows, rows)).astype(jnp.int16))

    def fill(j, carry):
        wanted = (jnp.broadcast_to(packed[pl.ds(j, 1), :], (rows, rows)).T - lane).astype(jnp.int16)
        row = pl.multiple_of(j * rows, rows)
        for b, begin in enumerate(starts):
            chosen[pl.ds(row, rows), b * rows : (b + 1) * rows] = jnp.where(
                wanted == begin, jnp.bfloat16(1), jnp.bfloat16(0)
            )
        if with_halo:
            first = jnp.where(wanted == 0, jnp.bfloat16(1), jnp.bfloat16(0))
            both = jnp.concatenate([halo_w[h] for h in range(halo_w.shape[0])], axis=1)
            chosen[pl.ds(row, rows), len(starts) * rows :] = jnp.dot(
                first, both, preferred_element_type=jnp.float32
            ).astype(jnp.bfloat16)
        return carry

    for j in range(blocks):
        fill(j, 0)


def choose(steps, places, packed, halo_w=None):
    extra = [] if halo_w is None else [halo_w]
    blocks, rows = packed.shape[0] - 8, packed.shape[1]
    columns = len(steps) * places * rows + sum(h.shape[0] * h.shape[1] for h in extra)
    shape = jax.ShapeDtypeStruct((blocks * rows, columns), jnp.bfloat16)
    return pl.pallas_call(
        functools.partial(choose_kernel, steps, bool(extra), places),
        out_shape=shape,
        in_specs=[VMEM] * (1 + len(extra)),
        out_specs=VMEM,
        compiler_params=pltpu.CompilerParams(
            vmem_limit_bytes=nbytes(packed, shape, *extra) + MARGIN
        ),
        cost_estimate=pl.CostEstimate(
            flops=shape.size, bytes_accessed=nbytes(shape), transcendentals=0
        ),
        name="choose",
    )(packed, *extra)


def place_kernel(steps, share, own, other, rim, *refs):
    outs = refs[-len(steps) :]
    parts = refs[: -len(steps)]
    me = lax.axis_index("dom")
    rows = [pl.multiple_of(jnp.bitwise_xor(me, step) * share, share) for step in steps]
    depth = parts[0].shape[0] // 2
    for side, matrix in enumerate((own, other)):
        stack = [part[side * depth : (side + 1) * depth] for part in parts]
        if side == 0:
            stack.append(rim[...])
        total = jnp.dot(
            jnp.concatenate([matrix[pl.ds(row, share)] for row in rows], axis=0),
            jnp.concatenate(stack, axis=0),
            preferred_element_type=jnp.float32,
        )
        for i, out in enumerate(outs):
            out[side * share : (side + 1) * share] = total[i * share : (i + 1) * share].astype(
                out.dtype
            )


def place(steps, share, own, other, rim, parts):
    width = rim.shape[1]
    shapes = [jax.ShapeDtypeStruct((2 * share, width), jnp.bfloat16)] * len(steps)
    return pl.pallas_call(
        functools.partial(place_kernel, steps, share),
        out_shape=shapes,
        in_specs=[VMEM] * (3 + len(parts)),
        out_specs=[VMEM] * len(shapes),
        compiler_params=pltpu.CompilerParams(
            vmem_limit_bytes=nbytes(own, other, rim, *parts, *shapes) + MARGIN
        ),
        cost_estimate=pl.CostEstimate(
            flops=own.size * width * 2, bytes_accessed=nbytes(own), transcendentals=0
        ),
        name="place",
    )(own, other, rim, *parts)


def join_kernel(count, *refs):
    chunks = refs[:count]
    out = refs[count]
    share = chunks[0].shape[0] // 2
    me = lax.axis_index("dom")
    for step in range(count):
        row = pl.multiple_of(jnp.bitwise_xor(me, step) * share, share)
        pair = chunks[step ^ (count // 2)]
        total = chunks[step][:share].astype(jnp.float32) + pair[share:].astype(jnp.float32)
        out[pl.ds(row, share)] = total.astype(out.dtype)


def join(chunks):
    count = len(chunks)
    share, width = chunks[0].shape[0] // 2, chunks[0].shape[1]
    return pl.pallas_call(
        functools.partial(join_kernel, count),
        out_shape=jax.ShapeDtypeStruct((share * count, width), chunks[0].dtype),
        in_specs=[VMEM] * count,
        out_specs=VMEM,
        compiler_params=pltpu.CompilerParams(vmem_limit_bytes=2 * nbytes(*chunks) + MARGIN),
        name="join",
    )(*chunks)


def near_steps(count):
    half = count // 2
    return [half - 1] + list(range(1, half - 1))


def on_device(
    donors, send_block, send_count, send_target, target_block, weights, halo_weights, permute
):
    block_rows = weights.shape[-1]
    rim_rows = halo_weights.shape[2] * block_rows
    count = lax.axis_size("dom")
    slabs = lax.axis_size("slab")
    half = count // 2
    share = permute.shape[-1] // count
    tables = send_block[0, 0], send_count[0, 0], send_target[0, 0]
    places = target_block.shape[-1]
    near = near_steps(count)
    order = permute[0, 0].reshape(-1, block_rows)
    *formed, own_part, rim, packed = form_parts(
        near + [0], tables, order, target_block[0, 0].T, donors, weights[0, 0], rim_rows
    )
    arrived = [swap(part, step) for part, step in zip(formed, near)]
    other_packed = swap(packed, half)
    rim = lax.ppermute(rim, "slab", [(source, source + 1) for source in range(slabs - 1)])
    own = choose([0] + near, places, packed, halo_weights[0, 0])
    other = choose([0] + near, places, other_packed)
    parts = [own_part, *arrived]
    far_steps = [*range(half, count), half - 1, 1]
    far = place(far_steps, share, own, other, rim, parts)
    close_steps = [*range(2, half - 1), 0]
    close = place(close_steps, share, own, other, rim, parts)
    chunks = [None] * count
    chunks[0] = close[-1]
    for step, chunk in zip(far_steps + close_steps[:-1], far + close[:-1]):
        chunks[step] = swap(chunk, step)
    return join(chunks)


def solution(mesh):
    return jax.shard_map(
        on_device,
        mesh=mesh,
        in_specs=(
            P(("slab", "dom"), None),
            P("slab", "dom", None, None),
            P("slab", "dom", None),
            P("slab", "dom", None, None),
            P("slab", "dom", None, None),
            P("slab", "dom", None, None, None, None),
            P("slab", "dom", None, None, None),
            P("slab", "dom", None),
        ),
        out_specs=P(("slab", "dom"), None),
        check_vma=False,
    )
```
